32 devices in a mesh: region: 2 (over x), row: 4 (over y, core), col: 4 (over z).
Axes of the slice: x: 2, y: 2, z: 4, core: 2. Of those that a mesh axis runs over, the one named last changes fastest.
Arguments:
- queries: bfloat16 [256, 32, 768], P(('region', 'row'), 'col'), parts along dimension 0, may hold values from -16 to 16
- key_states: bfloat16 [256, 32, 768], P(('region', 'row'), 'col'), parts along dimension 0, may hold values from -16 to 16
- value_states: bfloat16 [256, 32, 768], P(('region', 'row'), 'col'), parts along dimension 0, may hold values from -6 to 6
- out_grad: bfloat16 [256, 32, 768], P(('region', 'row'), 'col'), parts along dimension 0, may hold values from -6 to 6
- tissue: int32 [32, 4], P('region'), parts along dimension 0, may hold values from 0 to 1, as said below
- slide_id: int32 [32, 4], P('region'), parts along dimension 0, may hold values from 0 to 2, never falling along the last dimension, each value on 1 to 2 neighbouring positions
Outputs:
- attended: bfloat16 [256, 32, 768], P(('region', 'row'), 'col'), parts along dimension 0
- query_grad: bfloat16 [256, 32, 768], P(('region', 'row'), 'col'), parts along dimension 0
- key_grad: bfloat16 [256, 32, 768], P(('region', 'row'), 'col'), parts along dimension 0
- value_grad: bfloat16 [256, 32, 768], P(('region', 'row'), 'col'), parts along dimension 0
The draws below stay inside these ranges and needn't reach their ends.
There are 2 independent parts, one for each index of `region`. The reference program is written for one: setup_inputs(seed, part) draws one part's arguments, and reference() takes and returns one part's arrays. A program takes and returns all parts, laid end to end along the dimension named above; each array names one. Nothing has to cross between parts.
Inputs may be any that keep to these rules, and one draw needn't show every extreme that they name: 1 marks a block of tissue.
All inputs are finite; a program needn't handle non-finite values.
Results may differ from the reference program's by a relative error of at most 0.015.
Values may be sent and summed in bfloat16 or wider, within the bound.
A program may use at most 64 MiB of HBM per device.

```python
import math
import jax
import jax.numpy as jnp
import numpy as np
from jax import lax

D = 768
HEADS = 12
H = 128
W = 32
HB = 16
WB = 4


def draw_pair(key, part):
    base = jax.random.fold_in(key, 91)
    keys_list = jax.random.split(base, 2)
    full_shape = (H, W, D)
    query_vals = jnp.clip(jax.random.normal(keys_list[0], full_shape, jnp.float32), -6.0, 6.0)
    key_vals = jnp.clip(jax.random.normal(keys_list[1], full_shape, jnp.float32), -6.0, 6.0)
    return (query_vals, key_vals)


def draw_queries(key, part):
    return draw_pair(key, part)[0].astype(jnp.bfloat16)


def draw_key_states(key, part):
    return draw_pair(key, part)[1].astype(jnp.bfloat16)


def draw_tissue(key, part):
    keys_list = jax.random.split(jax.random.fold_in(key, 17), 2)
    levels = jax.random.randint(keys_list[0], (HB // 4 + 1, WB // 4 + 1), 1, 5)
    coverage = jnp.repeat(jnp.repeat(levels, 4, axis=0), 4, axis=1)[:HB, :WB]
    lottery = jax.random.randint(keys_list[1], (HB, WB), 0, 4)
    return (lottery < coverage).astype(jnp.int32)


def shard_levels(key, extent, shards, least, top_value):
    def one(position, parts):
        steps = jax.random.uniform(jax.random.fold_in(jax.random.fold_in(key, 6), position), (parts,), jnp.float32, least / len(shards), top_value / len(shards))
        return jnp.repeat(jnp.exp(steps), extent[position] // parts).reshape((-1,) + (1,) * (len(extent) - position - 1))

    loudness = one(*shards[0])
    for cut in shards[1:]:
        loudness = loudness * one(*cut)
    return loudness


def length_profile(count, total, most, lean):
    loads = [(1 << 20) // math.isqrt(grade ** lean) + 1 for grade in range(2, count + 1)]
    surplus, given = total - most - (count - 1), [1] * (count - 1)
    while surplus > 0:
        movable = [i for i in range(count - 1) if given[i] < most]
        mass, left = sum([loads[i] for i in movable]), surplus
        for i in movable:
            more = min(most - given[i], max(1, left * loads[i] // mass), surplus)
            given[i] = given[i] + more
            surplus = surplus - more
    return np.array([most] + given)


def uneven_parts(stream_key, amount, total, most, lean):
    if amount == 2:
        one = jax.random.randint(stream_key, (), max(1, total - most), min(most, total - 1) + 1)
        return jnp.stack([one, total - one])
    tallies = jnp.asarray(length_profile(amount, total, most, lean), jnp.int32)
    couples = (amount - 1) // 2
    giver, receiver = tallies[1:1 + 2 * couples:2], tallies[2:2 + 2 * couples:2]
    slack = jnp.minimum(giver - 1, most - receiver)
    shifted = jax.random.randint(jax.random.fold_in(stream_key, 1), (couples,), 0, 1 << 20) % (slack + 1)
    tallies = tallies.at[1:1 + 2 * couples:2].set(giver - shifted).at[2:2 + 2 * couples:2].set(receiver + shifted)
    return tallies[jax.random.permutation(jax.random.fold_in(stream_key, 2), amount)]


def noise(stream_key, shape, scale, reach, cuts=(), kind=jnp.bfloat16):
    result = jax.random.normal(stream_key, shape, jnp.float32) * scale
    if len(cuts) > 0:
        result = shard_levels(stream_key, shape, cuts, -0.22, 0.18) * result
    return jnp.clip(result, min=-reach, max=reach).astype(kind)


def setup_inputs(seed: int = 0, part: int = 0) -> dict:
    keys = jax.random.split(jax.random.key(seed), 7)
    own_keys = jax.random.split(jax.random.fold_in(keys[6], part), 7)
    return {
        "queries": draw_queries(jax.random.fold_in(jax.random.fold_in(keys[6], part), 71), part),
        "key_states": draw_key_states(jax.random.fold_in(jax.random.fold_in(keys[6], part), 71), part),
        "value_states": noise(own_keys[2], (H, W, D), 1.0, 6.0, ((0, 4), (1, 4))),
        "out_grad": noise(own_keys[3], (H, W, D), 1.0, 6.0, ((0, 4), (1, 4))),
        "tissue": draw_tissue(jax.random.fold_in(jax.random.fold_in(keys[6], part), 71), part),
        "slide_id": jax.vmap(lambda own: jnp.searchsorted(jnp.cumsum(uneven_parts(own, 3, WB, WB // 2, 0)), jnp.arange(WB), side="right"))(jax.random.split(own_keys[5], HB)).reshape((HB, WB)).astype(jnp.int32),
    }


def per_head(former, second):
    height, breadth, feature = former.shape
    product = former.astype(jnp.float32) * second.astype(jnp.float32)
    return jnp.sum(product.reshape(height, breadth, HEADS, feature // HEADS), axis=3)


def spread(head_values, values_in):
    height, breadth, feature = values_in.shape
    expanded = head_values.astype(jnp.float32)[..., None] * values_in.astype(jnp.float32).reshape(height, breadth, HEADS, feature // HEADS)
    return expanded.reshape(height, breadth, feature)


def reference(queries, key_states, value_states, out_grad, tissue, slide_id):
    height, breadth, feature = queries.shape
    score_scale = 1.0 / (feature // HEADS) ** 0.5
    tissue_tok = jnp.repeat(jnp.repeat(tissue, 8, axis=0), 8, axis=1)
    slide_tok = jnp.repeat(jnp.repeat(slide_id, 8, axis=0), 8, axis=1)
    tissue_pad = jnp.pad(tissue_tok, 3)
    slide_pad = jnp.pad(slide_tok, 3, constant_values=-1)
    spatial = ((3, 3), (3, 3), (0, 0))
    key_pad = jnp.pad(key_states, spatial)
    value_pad = jnp.pad(value_states, spatial)
    offsets = jnp.arange(49, dtype=jnp.int32)
    zero_index = jnp.zeros((), jnp.int32)

    def window_slice(array, offset):
        return lax.dynamic_slice(array, (offset // 7, offset % 7, zero_index), (height, breadth, feature))

    def label_slice(array, offset):
        return lax.dynamic_slice(array, (offset // 7, offset % 7), (height, breadth))

    def allowed_at(offset):
        same_slide = (tissue_tok == 1) & (label_slice(tissue_pad, offset) == 1) & (slide_tok == label_slice(slide_pad, offset))
        return same_slide | (offset == 24)

    def scores_at(offset):
        return per_head(queries, window_slice(key_pad, offset)) * score_scale

    scores = lax.map(scores_at, offsets)
    allowed = lax.map(allowed_at, offsets)[..., None]
    row_top = jnp.max(jnp.where(allowed, scores, -jnp.inf), axis=0)
    row_total = jnp.sum(jnp.exp(jnp.where(allowed, scores - row_top, -jnp.inf)), axis=0)
    log_total = row_top + jnp.log(row_total)
    weights = jnp.exp(jnp.where(allowed, scores - log_total, -jnp.inf))
    soft_weights = weights.astype(jnp.bfloat16)

    def attend(running, offset):
        return running + spread(soft_weights[offset], window_slice(value_pad, offset)), None

    attended_sum = lax.scan(attend, jnp.zeros((height, breadth, feature), jnp.float32), offsets)[0]
    attended = attended_sum.astype(jnp.bfloat16)
    row_delta = per_head(out_grad, attended)

    def backward(running, offset):
        query_acc, key_acc, value_acc = running
        prob_grad = per_head(out_grad, window_slice(value_pad, offset))
        score_grad = (weights[offset] * (prob_grad - row_delta) * score_scale).astype(jnp.bfloat16)
        query_acc = query_acc + spread(score_grad, window_slice(key_pad, offset))
        corner = (offset // 7, offset % 7, zero_index)
        key_acc = lax.dynamic_update_slice(key_acc, window_slice(key_acc, offset) + spread(score_grad, queries), corner)
        value_acc = lax.dynamic_update_slice(value_acc, window_slice(value_acc, offset) + spread(soft_weights[offset], out_grad), corner)
        return (query_acc, key_acc, value_acc), None

    start_grads = (jnp.zeros((height, breadth, feature), jnp.float32),
                   jnp.zeros((height + 6, breadth + 6, feature), jnp.float32),
                   jnp.zeros((height + 6, breadth + 6, feature), jnp.float32))
    query_acc, key_acc, value_acc = lax.scan(backward, start_grads, offsets)[0]
    query_grad = query_acc.astype(jnp.bfloat16)
    key_grad = key_acc[3:height + 3, 3:breadth + 3].astype(jnp.bfloat16)
    value_grad = value_acc[3:height + 3, 3:breadth + 3].astype(jnp.bfloat16)
    return (attended, query_grad, key_grad, value_grad)
```

```python
import functools

import jax
import jax.numpy as jnp
import numpy as np
from jax import lax
from jax.experimental import pallas as pl
from jax.experimental.pallas import tpu as pltpu
from jax.sharding import PartitionSpec as P

HEADS = 12
LABEL = 8
REACH = 3
RIM = 4
PACK = 16
MESH = pl.DeviceIdType.MESH
BF16 = jnp.bfloat16
F32 = jnp.float32


def edge_places(rows):
    places = [None] * (2 * PACK + REACH * rows)
    for t in range(RIM * REACH):
        places[t] = (t // REACH - RIM, t % REACH)
        places[PACK + REACH * rows + t] = (rows + t // REACH, t % REACH)
    for t in range(REACH * rows):
        places[PACK + t] = (t // REACH, t % REACH)
    return places


def strip_start(block, rows):
    return min((LABEL * REACH * block + PACK - RIM * REACH) // PACK * PACK, REACH * rows + 2 * PACK - 64)


def edge_picks(rows, cols):
    places = edge_places(rows)
    picks = np.zeros((2, len(places), rows * cols), np.float32)
    for slot, place in enumerate(places):
        if place is not None:
            row, j = place
            picks[0, slot, (row % rows) * cols + j] = 1
            picks[1, slot, (row % rows) * cols + cols - REACH + j] = 1
    return picks.reshape(2 * len(places), rows * cols)


def pair_codes(rows, cols):
    places = edge_places(rows)
    blocks = rows // LABEL
    codes = np.full((blocks, LABEL * cols, 128 + 128), -1, np.float32)
    for b in range(blocks):
        keys = [((LABEL * cols * b + s) // cols - RIM, s % cols) for s in range(128)]
        first = strip_start(b, rows)
        for shift in (-REACH, cols):
            for s in range(64):
                place = places[first + s]
                keys.append(None if place is None else (place[0], place[1] + shift))
        for q in range(LABEL * cols):
            row, col = LABEL * b + q // cols, q % cols
            for n, key in enumerate(keys):
                if key is None or abs(key[0] - row) > REACH or abs(key[1] - col) > REACH:
                    continue
                if key == (row, col):
                    codes[b, q, n] = 9
                else:
                    codes[b, q, n] = (key[0] // LABEL - b + 1) * 3 + key[1] // LABEL + 1
    return codes


def dot(a, b, contract):
    return lax.dot_general(a, b, ((contract[:1], contract[1:]), ((), ())), preferred_element_type=F32)


def kernel(
    sizes,
    q_ref, k_ref, v_ref, do_ref, tissue_ref, slide_ref, code_ref, pick_ref, place_ref,
    att_ref, dq_ref, dk_ref, dv_ref,
    own, strip, edge, grow, gstrip, rrow, redge, acc, sacc, bias,
    send_sem, recv_sem, gsend_sem, grecv_sem,
):
    rows, cols, groups, width, depth, row_size, col_size = sizes
    tokens = rows * cols
    rim = RIM * cols
    side = REACH * rows
    slots = side + 2 * PACK
    blocks = rows // LABEL
    per_block = LABEL * cols
    stacked = width // depth
    region, row, col = lax.axis_index("region"), lax.axis_index("row"), lax.axis_index("col")

    top, mid, bottom = pl.ds(0, PACK), pl.ds(PACK, side), pl.ds(PACK + side, PACK)
    routes = []
    for source, dc in ((0, -1), (1, 1)):
        routes.append((0, dc, source, mid))
        routes.append((1, dc, source, top))
        routes.append((-1, dc, source, bottom))
    routes.append((-1, 0, 2, None))
    routes.append((1, 0, 3, None))

    def exists(dr, dc):
        good = None
        for at, d, size in ((row, dr, row_size), (col, dc, col_size)):
            if d:
                here = (at + d >= 0) if d < 0 else (at + d < size)
                good = here if good is None else good & here
        return good

    def device(dr, dc):
        return (region, row + dr, col + dc)

    def out_copy(g, n, target):
        dr, dc, source, part = routes[n]
        if source < 2:
            src, dst = edge.at[source, g, :, part], strip.at[1 - source, g, :, part]
        elif source == 2:
            src, dst = own.at[g, :, pl.ds(rim, rim)], own.at[g, :, pl.ds(rim + tokens, rim)]
        else:
            src, dst = own.at[g, :, pl.ds(tokens, rim)], own.at[g, :, pl.ds(0, rim)]
        return pltpu.make_async_remote_copy(
            src_ref=src, dst_ref=dst, send_sem=send_sem.at[g, n], recv_sem=recv_sem.at[g, n],
            device_id=target, device_id_type=MESH)

    def back_copy(g, n, target):
        dr, dc, source, part = routes[n]
        if source < 2:
            src, dst = gstrip.at[1 - source, g, :, part], redge.at[source, g, :, part]
        else:
            src, dst = grow.at[3 - source, g], rrow.at[source - 2, g]
        return pltpu.make_async_remote_copy(
            src_ref=src, dst_ref=dst, send_sem=gsend_sem.at[g, n], recv_sem=grecv_sem.at[g, n],
            device_id=target, device_id_type=MESH)

    zero_rim = jnp.zeros((groups, 2, rim, width), BF16)
    own[:, :, pl.ds(0, rim)] = zero_rim
    own[:, :, pl.ds(rim + tokens, rim)] = zero_rim
    strip[...] = jnp.zeros(strip.shape, BF16)
    redge[...] = jnp.zeros(redge.shape, BF16)
    rrow[...] = jnp.zeros(rrow.shape, BF16)

    barrier = pltpu.get_barrier_semaphore()
    around = jnp.int32(0)
    for dr in (-1, 0, 1):
        for dc in (-1, 0, 1):
            if dr or dc:
                good = exists(dr, dc)
                around = around + good.astype(jnp.int32)

                @pl.when(good)
                def _(dr=dr, dc=dc):
                    pl.semaphore_signal(barrier, inc=1, device_id=device(dr, dc), device_id_type=MESH)

    def stage(g, carry):
        lanes = pl.ds(pl.multiple_of(g * width, width), width)
        for i, ref in enumerate((k_ref, v_ref)):
            block = ref[:, lanes]
            own[g, i, pl.ds(rim, tokens)] = block
            picked = dot(pick_ref[...], block, (1, 0)).astype(BF16)
            edge[0, g, i] = picked[:slots]
            edge[1, g, i] = picked[slots:]
        return carry

    lax.fori_loop(0, groups, stage, 0)
    pl.semaphore_wait(barrier, around)

    def send(g, carry):
        for n, (dr, dc, _, _) in enumerate(routes):
            @pl.when(exists(dr, dc))
            def _(n=n, dr=dr, dc=dc):
                out_copy(g, n, device(dr, dc)).start()
        return carry

    lax.fori_loop(0, groups, send, 0)

    def label(r, c):
        r_all, c_all = tissue_ref.shape
        inside = (r >= 0) & (r < r_all) & (c >= 0) & (c < c_all)
        r, c = jnp.clip(r, 0, r_all - 1), jnp.clip(c, 0, c_all - 1)
        return jnp.where(inside & (tissue_ref[r, c] == 1), slide_ref[r, c] + 1, 0)

    labels = [[label(row * blocks + i - 1, col + j - 1) for j in range(3)] for i in range(blocks + 2)]
    for b in range(blocks):
        code = code_ref[b]
        mine = labels[b + 1][1]
        level = jnp.where(code == 9, 0.0, -1e30)
        for n in range(9):
            value = jnp.where((mine > 0) & (labels[b + n // 3][n % 3] == mine), 0.0, -1e30)
            level = jnp.where(code == n, value, level)
        bias[b] = level

    lane_head = lax.broadcasted_iota(jnp.int32, (per_block, width), 1) // depth

    def stack(block):
        zero = jnp.zeros_like(block)
        return jnp.concatenate([jnp.where(lane_head == h, block, zero) for h in range(stacked)], axis=0)

    def unstack(full):
        result = full[:per_block]
        for h in range(1, stacked):
            result = jnp.where(lane_head == h, full[h * per_block:(h + 1) * per_block], result)
        return result

    def compute(g, carry):
        for n, (dr, dc, _, _) in enumerate(routes):
            @pl.when(exists(-dr, -dc))
            def _(n=n, dr=dr, dc=dc):
                out_copy(g, n, device(-dr, -dc)).wait_recv()
        lanes = pl.ds(pl.multiple_of(g * width, width), width)
        acc[g] = jnp.zeros(acc.shape[1:], F32)
        sacc[...] = jnp.zeros(sacc.shape, F32)
        for b in range(blocks):
            mine = pl.ds(b * per_block, per_block)
            near = pl.ds(b * per_block, 128)
            far = pl.ds(strip_start(b, rows), 64)
            scale = 1.0 / depth ** 0.5
            q = stack((q_ref[mine, lanes].astype(F32) * scale).astype(BF16))
            grad_block = do_ref[mine, lanes]
            do = stack(grad_block)
            keys, values = (
                jnp.concatenate([own[g, i, near], strip[0, g, i, far], strip[1, g, i, far]], axis=0)
                for i in range(2))
            level = bias[b]
            scores = dot(q, keys, (1, 1)) + jnp.concatenate([level] * stacked, axis=0)
            highest = jnp.max(scores, axis=1, keepdims=True)
            powers = jnp.exp(scores - highest)
            total = jnp.sum(powers, axis=1, keepdims=True)
            weights = powers * (1.0 / total)
            soft = weights.astype(BF16)
            attended = unstack(dot(soft, values, (1, 0))).astype(BF16)
            att_ref[mine, lanes] = attended
            product = grad_block.astype(F32) * attended.astype(F32)
            delta = jnp.concatenate(
                [jnp.sum(jnp.where(lane_head == h, product, 0.0), axis=1, keepdims=True) for h in range(stacked)],
                axis=0)
            prob_grad = dot(do, values, (1, 1))
            score_grad = (weights * (prob_grad - delta)).astype(BF16)
            dq_ref[mine, lanes] = (unstack(dot(score_grad, keys, (1, 0))) * scale).astype(BF16)
            for i, part in enumerate((dot(score_grad, q, (0, 0)), dot(soft, do, (0, 0)))):
                acc[g, i, near] += part[:128]
                sacc[0, i, far] += part[128:192]
                sacc[1, i, far] += part[192:]
        grow[0, g] = acc[g, :, pl.ds(0, rim)].astype(BF16)
        grow[1, g] = acc[g, :, pl.ds(rim + tokens, rim)].astype(BF16)
        gstrip[:, g] = sacc[...].astype(BF16)
        for n, (dr, dc, _, _) in enumerate(routes):
            @pl.when(exists(-dr, -dc))
            def _(n=n, dr=dr, dc=dc):
                back_copy(g, n, device(-dr, -dc)).start()
        return carry

    lax.fori_loop(0, groups, compute, 0)

    def finish(g, carry):
        for n, (dr, dc, _, _) in enumerate(routes):
            @pl.when(exists(dr, dc))
            def _(n=n, dr=dr, dc=dc):
                out_copy(g, n, device(dr, dc)).wait_send()
                back_copy(g, n, device(dr, dc)).wait_recv()
        lanes = pl.ds(pl.multiple_of(g * width, width), width)
        for i, ref in enumerate((dk_ref, dv_ref)):
            edges = jnp.concatenate([redge[0, g, i], redge[1, g, i]], axis=0)
            acc[g, i, pl.ds(rim, rim)] += rrow[0, g, i].astype(F32)
            acc[g, i, pl.ds(tokens, rim)] += rrow[1, g, i].astype(F32)
            total = acc[g, i, pl.ds(rim, tokens)] + dot(place_ref[...], edges, (1, 0))
            ref[:, lanes] = total.astype(BF16)
        for n, (dr, dc, _, _) in enumerate(routes):
            @pl.when(exists(-dr, -dc))
            def _(n=n, dr=dr, dc=dc):
                back_copy(g, n, device(-dr, -dc)).wait_send()
        return carry

    lax.fori_loop(0, groups, finish, 0)


def local(queries, key_states, value_states, out_grad, tissue, slide_id):
    rows, cols, feature = queries.shape
    depth = feature // HEADS
    stacked = 4
    width = stacked * depth
    groups = feature // width
    tokens = rows * cols
    rim = RIM * cols
    slots = REACH * rows + 2 * PACK
    sizes = (rows, cols, groups, width, depth, lax.axis_size("row"), lax.axis_size("col"))
    picks = edge_picks(rows, cols)
    flat = [a.reshape(tokens, feature) for a in (queries, key_states, value_states, out_grad)]
    vmem = pl.BlockSpec(memory_space=pltpu.VMEM)
    smem = pl.BlockSpec(memory_space=pltpu.SMEM)
    outs = pl.pallas_call(
        functools.partial(kernel, sizes),
        out_shape=[jax.ShapeDtypeStruct((tokens, feature), BF16)] * 4,
        in_specs=[vmem] * 4 + [smem] * 2 + [vmem] * 3,
        out_specs=[vmem] * 4,
        scratch_shapes=[
            pltpu.VMEM((groups, 2, tokens + 2 * rim, width), BF16),
            pltpu.VMEM((2, groups, 2, slots, width), BF16),
            pltpu.VMEM((2, groups, 2, slots, width), BF16),
            pltpu.VMEM((2, groups, 2, rim, width), BF16),
            pltpu.VMEM((2, groups, 2, slots, width), BF16),
            pltpu.VMEM((2, groups, 2, rim, width), BF16),
            pltpu.VMEM((2, groups, 2, slots, width), BF16),
            pltpu.VMEM((groups, 2, tokens + 2 * rim, width), F32),
            pltpu.VMEM((2, 2, slots, width), F32),
            pltpu.VMEM((rows // LABEL, LABEL * cols, 256), F32),
            pltpu.SemaphoreType.DMA((groups, 8)),
            pltpu.SemaphoreType.DMA((groups, 8)),
            pltpu.SemaphoreType.DMA((groups, 8)),
            pltpu.SemaphoreType.DMA((groups, 8)),
        ],
        compiler_params=pltpu.CompilerParams(
            collective_id=0, has_side_effects=True, vmem_limit_bytes=48 * 2 ** 20),
        name="window_attention",
    )(
        *flat, tissue, slide_id,
        jnp.asarray(pair_codes(rows, cols)),
        jnp.asarray(picks, BF16),
        jnp.asarray(picks.T, BF16),
    )
    return tuple(a.reshape(rows, cols, feature) for a in outs)


def solution(mesh):
    tile = P(("region", "row"), "col", None)
    table = P("region", None)
    return jax.shard_map(
        local,
        mesh=mesh,
        in_specs=(tile,) * 4 + (table,) * 2,
        out_specs=(tile,) * 4,
        check_vma=False,
    )
```

```python
import functools

import jax
import jax.numpy as jnp
import numpy as np
from jax import lax
from jax.experimental import pallas as pl
from jax.experimental.pallas import tpu as pltpu
from jax.sharding import PartitionSpec as P

HEADS = 12
LABEL = 8
REACH = 3
RIM = 4
PACK = 16
MESH = pl.DeviceIdType.MESH
BF16 = jnp.bfloat16
F32 = jnp.float32


def edge_places(rows):
    places = [None] * (2 * PACK + REACH * rows)
    for t in range(RIM * REACH):
        places[t] = (t // REACH - RIM, t % REACH)
        places[PACK + REACH * rows + t] = (rows + t // REACH, t % REACH)
    for t in range(REACH * rows):
        places[PACK + t] = (t // REACH, t % REACH)
    return places


def strip_start(block, rows):
    return min((LABEL * REACH * block + PACK - RIM * REACH) // PACK * PACK, REACH * rows + 2 * PACK - 64)


def edge_picks(rows, cols):
    places = edge_places(rows)
    picks = np.zeros((2, len(places), rows * cols), np.float32)
    for slot, place in enumerate(places):
        if place is not None:
            row, j = place
            picks[0, slot, (row % rows) * cols + j] = 1
            picks[1, slot, (row % rows) * cols + cols - REACH + j] = 1
    return picks.reshape(2 * len(places), rows * cols)


def pair_codes(rows, cols):
    places = edge_places(rows)
    blocks = rows // LABEL
    codes = np.full((blocks, LABEL * cols, 128 + 128), -1, np.float32)
    for b in range(blocks):
        keys = [((LABEL * cols * b + s) // cols - RIM, s % cols) for s in range(128)]
        first = strip_start(b, rows)
        for shift in (-REACH, cols):
            for s in range(64):
                place = places[first + s]
                keys.append(None if place is None else (place[0], place[1] + shift))
        for q in range(LABEL * cols):
            row, col = LABEL * b + q // cols, q % cols
            for n, key in enumerate(keys):
                if key is None or abs(key[0] - row) > REACH or abs(key[1] - col) > REACH:
                    continue
                if key == (row, col):
                    codes[b, q, n] = 9
                else:
                    codes[b, q, n] = (key[0] // LABEL - b + 1) * 3 + key[1] // LABEL + 1
    return np.tile(codes.transpose(0, 2, 1), (1, 1, 2))


def dot(a, b, contract):
    return lax.dot_general(a, b, ((contract[:1], contract[1:]), ((), ())), preferred_element_type=F32)


def kernel(
    sizes,
    q_hbm, k_hbm, v_hbm, do_hbm, tissue_ref, slide_ref, code_hbm, pick_hbm, place_hbm,
    att_ref, dq_ref, dk_ref, dv_ref,
    q_ref, do_ref, code_ref, pick_ref, place_ref, own, strip, edge, grow, gstrip, rrow, redge, acc, sacc, bias,
    send_sem, recv_sem, gsend_sem, grecv_sem, load_sem, table_sem,
):
    rows, cols, groups, width, depth, row_size, col_size = sizes
    tokens = rows * cols
    rim = RIM * cols
    side = REACH * rows
    slots = side + 2 * PACK
    blocks = rows // LABEL
    per_block = LABEL * cols
    stacked = width // depth
    region, row, col = lax.axis_index("region"), lax.axis_index("row"), lax.axis_index("col")

    top, mid, bottom = pl.ds(0, PACK), pl.ds(PACK, side), pl.ds(PACK + side, PACK)
    routes = []
    for source, dc in ((0, -1), (1, 1)):
        routes.append((0, dc, source, mid))
        routes.append((1, dc, source, top))
        routes.append((-1, dc, source, bottom))
    routes.append((-1, 0, 2, None))
    routes.append((1, 0, 3, None))

    def exists(dr, dc):
        good = None
        for at, d, size in ((row, dr, row_size), (col, dc, col_size)):
            if d:
                here = (at + d >= 0) if d < 0 else (at + d < size)
                good = here if good is None else good & here
        return good

    def device(dr, dc):
        return (region, row + dr, col + dc)

    def out_copy(g, n, target):
        dr, dc, source, part = routes[n]
        if source < 2:
            src, dst = edge.at[source, g, :, part], strip.at[1 - source, g, :, part]
        elif source == 2:
            src, dst = own.at[g, :, pl.ds(rim, rim)], own.at[g, :, pl.ds(rim + tokens, rim)]
        else:
            src, dst = own.at[g, :, pl.ds(tokens, rim)], own.at[g, :, pl.ds(0, rim)]
        return pltpu.make_async_remote_copy(
            src_ref=src, dst_ref=dst, send_sem=send_sem.at[g, n], recv_sem=recv_sem.at[g, n],
            device_id=target, device_id_type=MESH)

    def back_copy(g, n, target):
        dr, dc, source, part = routes[n]
        if source < 2:
            src, dst = gstrip.at[1 - source, g, :, part], redge.at[source, g, :, part]
        else:
            src, dst = grow.at[3 - source, g], rrow.at[source - 2, g]
        return pltpu.make_async_remote_copy(
            src_ref=src, dst_ref=dst, send_sem=gsend_sem.at[g, n], recv_sem=grecv_sem.at[g, n],
            device_id=target, device_id_type=MESH)

    def load(g, n):
        lanes = pl.ds(g * width, width)
        if n < 2:
            src, dst = (k_hbm, v_hbm)[n], own.at[g, n, pl.ds(rim, tokens)]
        else:
            src, dst = (q_hbm, do_hbm)[n - 2], (q_ref, do_ref)[n - 2].at[g]
        return pltpu.make_async_copy(src.at[:, lanes], dst, load_sem.at[g, n])

    tables = [
        pltpu.make_async_copy(src, dst, table_sem.at[n])
        for n, (src, dst) in enumerate(((pick_hbm, pick_ref), (code_hbm, code_ref), (place_hbm, place_ref)))]
    tables[0].start()
    for g in range(groups):
        for n in range(2):
            load(g, n).start()
    tables[1].start()
    for g in range(groups):
        for n in range(2, 4):
            load(g, n).start()
    tables[2].start()

    zero_rim = jnp.zeros((groups, 2, rim, width), BF16)
    own[:, :, pl.ds(0, rim)] = zero_rim
    own[:, :, pl.ds(rim + tokens, rim)] = zero_rim
    strip[...] = jnp.zeros(strip.shape, BF16)
    redge[...] = jnp.zeros(redge.shape, BF16)
    rrow[...] = jnp.zeros(rrow.shape, BF16)

    barrier = pltpu.get_barrier_semaphore()
    around = jnp.int32(0)
    for dr in (-1, 0, 1):
        for dc in (-1, 0, 1):
            if dr or dc:
                good = exists(dr, dc)
                around = around + good.astype(jnp.int32)

                @pl.when(good)
                def _(dr=dr, dc=dc):
                    pl.semaphore_signal(barrier, inc=1, device_id=device(dr, dc), device_id_type=MESH)

    tables[0].wait()
    for g in range(groups):
        for i in range(2):
            load(g, i).wait()
            picked = dot(pick_ref[...], own[g, i, pl.ds(rim, tokens)], (1, 0)).astype(BF16)
            edge[0, g, i] = picked[:slots]
            edge[1, g, i] = picked[slots:]
        if g == 0:
            pl.semaphore_wait(barrier, around)
        for n, (dr, dc, _, _) in enumerate(routes):
            @pl.when(exists(dr, dc))
            def _(n=n, dr=dr, dc=dc):
                out_copy(g, n, device(dr, dc)).start()

    def label(r, c):
        c_all, r_all = tissue_ref.shape
        inside = (r >= 0) & (r < r_all) & (c >= 0) & (c < c_all)
        r, c = jnp.clip(r, 0, r_all - 1), jnp.clip(c, 0, c_all - 1)
        return jnp.where(inside & (tissue_ref[c, r] == 1), slide_ref[c, r] + 1, 0)

    labels = [[label(row * blocks + i - 1, col + j - 1) for j in range(3)] for i in range(blocks + 2)]
    tables[1].wait()
    for b in range(blocks):
        code = code_ref[b]
        mine = labels[b + 1][1]
        level = jnp.where(code == 9, 0.0, -1e30)
        for n in range(9):
            value = jnp.where((mine > 0) & (labels[b + n // 3][n % 3] == mine), 0.0, -1e30)
            level = jnp.where(code == n, value, level)
        bias[b] = level

    lane_head = lax.broadcasted_iota(jnp.int32, (per_block, width), 1) // depth

    def stack(block):
        zero = jnp.zeros_like(block)
        return jnp.concatenate([jnp.where(lane_head == h, block, zero) for h in range(stacked)], axis=0)

    def unstack(full):
        result = full[:per_block]
        for h in range(1, stacked):
            result = jnp.where(lane_head == h, full[h * per_block:(h + 1) * per_block], result)
        return result

    for g in range(groups):
        for n in range(2, 4):
            load(g, n).wait()
    tables[2].wait()

    def compute(g, carry):
        for n, (dr, dc, _, _) in enumerate(routes):
            @pl.when(exists(-dr, -dc))
            def _(n=n, dr=dr, dc=dc):
                out_copy(g, n, device(-dr, -dc)).wait_recv()
        lanes = pl.ds(pl.multiple_of(g * width, width), width)
        acc[g] = jnp.zeros(acc.shape[1:], F32)
        sacc[...] = jnp.zeros(sacc.shape, F32)
        for b in range(blocks):
            mine = pl.ds(b * per_block, per_block)
            near = pl.ds(b * per_block, 128)
            far = pl.ds(strip_start(b, rows), 64)
            scale = 1.0 / depth ** 0.5
            q = stack((q_ref[g, mine].astype(F32) * scale).astype(BF16))
            do = stack(do_ref[g, mine])
            keys, values = (
                jnp.concatenate([own[g, i, near], strip[0, g, i, far], strip[1, g, i, far]], axis=0)
                for i in range(2))
            scores = dot(keys, q, (1, 1)) + jnp.concatenate([bias[b]] * (stacked // 2), axis=1)
            highest = jnp.max(scores, axis=0, keepdims=True)
            powers = jnp.exp(scores - highest)
            total = jnp.sum(powers, axis=0, keepdims=True)
            weights = powers * (1.0 / total)
            soft = weights.astype(BF16)
            prob_grad = dot(values, do, (1, 1))
            delta = jnp.sum(weights * prob_grad, axis=0, keepdims=True)
            score_grad = (weights * (prob_grad - delta)).astype(BF16)
            att_ref[mine, lanes] = unstack(dot(soft, values, (0, 0))).astype(BF16)
            dq_ref[mine, lanes] = (unstack(dot(score_grad, keys, (0, 0))) * scale).astype(BF16)
            for i, part in enumerate((dot(score_grad, q, (1, 0)), dot(soft, do, (1, 0)))):
                acc[g, i, near] += part[:128]
                sacc[0, i, far] += part[128:192]
                sacc[1, i, far] += part[192:]
        grow[0, g] = acc[g, :, pl.ds(0, rim)].astype(BF16)
        grow[1, g] = acc[g, :, pl.ds(rim + tokens, rim)].astype(BF16)
        gstrip[:, g] = sacc[...].astype(BF16)
        for n, (dr, dc, _, _) in enumerate(routes):
            @pl.when(exists(-dr, -dc))
            def _(n=n, dr=dr, dc=dc):
                back_copy(g, n, device(-dr, -dc)).start()
        return carry

    lax.fori_loop(0, groups, compute, 0)

    def finish(g, carry):
        for n, (dr, dc, _, _) in enumerate(routes):
            @pl.when(exists(dr, dc))
            def _(n=n, dr=dr, dc=dc):
                out_copy(g, n, device(dr, dc)).wait_send()
                back_copy(g, n, device(dr, dc)).wait_recv()
        lanes = pl.ds(pl.multiple_of(g * width, width), width)
        for i, ref in enumerate((dk_ref, dv_ref)):
            edges = jnp.concatenate([redge[0, g, i], redge[1, g, i]], axis=0)
            acc[g, i, pl.ds(rim, rim)] += rrow[0, g, i].astype(F32)
            acc[g, i, pl.ds(tokens, rim)] += rrow[1, g, i].astype(F32)
            total = acc[g, i, pl.ds(rim, tokens)] + dot(place_ref[...], edges, (1, 0))
            ref[:, lanes] = total.astype(BF16)
        for n, (dr, dc, _, _) in enumerate(routes):
            @pl.when(exists(-dr, -dc))
            def _(n=n, dr=dr, dc=dc):
                back_copy(g, n, device(-dr, -dc)).wait_send()
        return carry

    lax.fori_loop(0, groups, finish, 0)


def write_out(*refs):
    copies = [pltpu.make_async_copy(refs[n], refs[4 + n], refs[8].at[n]) for n in range(4)]
    for copy in copies:
        copy.start()
    for copy in copies:
        copy.wait()


def local(queries, key_states, value_states, out_grad, tissue, slide_id):
    rows, cols, feature = queries.shape
    depth = feature // HEADS
    stacked = 4
    width = stacked * depth
    groups = feature // width
    tokens = rows * cols
    rim = RIM * cols
    slots = REACH * rows + 2 * PACK
    sizes = (rows, cols, groups, width, depth, lax.axis_size("row"), lax.axis_size("col"))
    picks = edge_picks(rows, cols)
    flat = [a.reshape(tokens, feature) for a in (queries, key_states, value_states, out_grad)]
    vmem = pl.BlockSpec(memory_space=pltpu.VMEM)
    smem = pl.BlockSpec(memory_space=pltpu.SMEM)
    hbm = pl.BlockSpec(memory_space=pltpu.HBM)
    blocks = rows // LABEL
    outs = pl.pallas_call(
        functools.partial(kernel, sizes),
        out_shape=[jax.ShapeDtypeStruct((tokens, feature), BF16)] * 4,
        in_specs=[hbm] * 4 + [smem] * 2 + [hbm] * 3,
        out_specs=[vmem] * 4,
        scratch_shapes=[
            pltpu.VMEM((groups, tokens, width), BF16),
            pltpu.VMEM((groups, tokens, width), BF16),
            pltpu.VMEM((blocks, 256, 2 * LABEL * cols), F32),
            pltpu.VMEM((2 * slots, tokens), BF16),
            pltpu.VMEM((tokens, 2 * slots), BF16),
            pltpu.VMEM((groups, 2, tokens + 2 * rim, width), BF16),
            pltpu.VMEM((2, groups, 2, slots, width), BF16),
            pltpu.VMEM((2, groups, 2, slots, width), BF16),
            pltpu.VMEM((2, groups, 2, rim, width), BF16),
            pltpu.VMEM((2, groups, 2, slots, width), BF16),
            pltpu.VMEM((2, groups, 2, rim, width), BF16),
            pltpu.VMEM((2, groups, 2, slots, width), BF16),
            pltpu.VMEM((groups, 2, tokens + 2 * rim, width), F32),
            pltpu.VMEM((2, 2, slots, width), F32),
            pltpu.VMEM((blocks, 256, 2 * LABEL * cols), F32),
            pltpu.SemaphoreType.DMA((groups, 8)),
            pltpu.SemaphoreType.DMA((groups, 8)),
            pltpu.SemaphoreType.DMA((groups, 8)),
            pltpu.SemaphoreType.DMA((groups, 8)),
            pltpu.SemaphoreType.DMA((groups, 4)),
            pltpu.SemaphoreType.DMA((3,)),
        ],
        compiler_params=pltpu.CompilerParams(
            collective_id=0, has_side_effects=True, vmem_limit_bytes=60 * 2 ** 20),
        name="window_attention",
    )(
        *flat, tissue.T, slide_id.T,
        jnp.asarray(pair_codes(rows, cols)),
        jnp.asarray(picks, BF16),
        jnp.asarray(picks.T, BF16),
    )
    outs = pl.pallas_call(
        write_out,
        out_shape=[jax.ShapeDtypeStruct((tokens, feature), BF16)] * 4,
        in_specs=[pl.BlockSpec(memory_space=pl.ANY)] * 4,
        out_specs=[hbm] * 4,
        scratch_shapes=[pltpu.SemaphoreType.DMA((4,))],
        name="write_out",
    )(*outs)
    return tuple(a.reshape(rows, cols, feature) for a in outs)


def solution(mesh):
    tile = P(("region", "row"), "col", None)
    table = P("region", None)
    return jax.shard_map(
        local,
        mesh=mesh,
        in_specs=(tile,) * 4 + (table,) * 2,
        out_specs=(tile,) * 4,
        check_vma=False,
    )
```

```python
import functools

import jax
import jax.numpy as jnp
import numpy as np
from jax import lax
from jax.experimental import pallas as pl
from jax.experimental.pallas import tpu as pltpu
from jax.sharding import PartitionSpec as P

HEADS = 12
LABEL = 8
REACH = 3
RIM = 4
PACK = 16
MESH = pl.DeviceIdType.MESH
BF16 = jnp.bfloat16
F32 = jnp.float32


def edge_places(rows):
    places = [None] * (2 * PACK + REACH * rows)
    for t in range(RIM * REACH):
        places[t] = (t // REACH - RIM, t % REACH)
        places[PACK + REACH * rows + t] = (rows + t // REACH, t % REACH)
    for t in range(REACH * rows):
        places[PACK + t] = (t // REACH, t % REACH)
    return places


def strip_start(block, rows):
    return min((LABEL * REACH * block + PACK - RIM * REACH) // PACK * PACK, REACH * rows + 2 * PACK - 64)


def edge_picks(rows, cols):
    places = edge_places(rows)
    picks = np.zeros((2, len(places), rows * cols), np.float32)
    for slot, place in enumerate(places):
        if place is not None:
            row, j = place
            picks[0, slot, (row % rows) * cols + j] = 1
            picks[1, slot, (row % rows) * cols + cols - REACH + j] = 1
    return picks.reshape(2 * len(places), rows * cols)


def pair_codes(rows, cols):
    places = edge_places(rows)
    blocks = rows // LABEL
    codes = np.full((blocks, LABEL * cols, 128 + 128), -1, np.float32)
    for b in range(blocks):
        keys = [((LABEL * cols * b + s) // cols - RIM, s % cols) for s in range(128)]
        first = strip_start(b, rows)
        for shift in (-REACH, cols):
            for s in range(64):
                place = places[first + s]
                keys.append(None if place is None else (place[0], place[1] + shift))
        for q in range(LABEL * cols):
            row, col = LABEL * b + q // cols, q % cols
            for n, key in enumerate(keys):
                if key is None or abs(key[0] - row) > REACH or abs(key[1] - col) > REACH:
                    continue
                if key == (row, col):
                    codes[b, q, n] = 9
                else:
                    codes[b, q, n] = (key[0] // LABEL - b + 1) * 3 + key[1] // LABEL + 1
    return np.tile(codes.transpose(0, 2, 1), (1, 1, 2))


def dot(a, b, contract):
    return lax.dot_general(a, b, ((contract[:1], contract[1:]), ((), ())), preferred_element_type=F32)


def kernel(
    sizes,
    q_hbm, k_hbm, v_hbm, do_hbm, tissue_hbm, slide_hbm, code_hbm, pick_hbm, place_hbm,
    att_ref, dq_ref, dk_ref, dv_ref,
    tissue_ref, slide_ref, q_ref, do_ref, code_ref, pick_ref, place_ref, own, strip, edge, grow, gstrip, rrow, redge, acc, sacc, bias,
    send_sem, recv_sem, gsend_sem, grecv_sem, load_sem, table_sem,
):
    rows, cols, groups, width, depth, row_size, col_size = sizes
    tokens = rows * cols
    rim = RIM * cols
    side = REACH * rows
    slots = side + 2 * PACK
    blocks = rows // LABEL
    per_block = LABEL * cols
    stacked = width // depth
    region, row, col = lax.axis_index("region"), lax.axis_index("row"), lax.axis_index("col")

    top, mid, bottom = pl.ds(0, PACK), pl.ds(PACK, side), pl.ds(PACK + side, PACK)
    routes = []
    for source, dc in ((0, -1), (1, 1)):
        routes.append((0, dc, source, mid))
        routes.append((1, dc, source, top))
        routes.append((-1, dc, source, bottom))
    routes.append((-1, 0, 2, None))
    routes.append((1, 0, 3, None))

    def exists(dr, dc):
        good = None
        for at, d, size in ((row, dr, row_size), (col, dc, col_size)):
            if d:
                here = (at + d >= 0) if d < 0 else (at + d < size)
                good = here if good is None else good & here
        return good

    def device(dr, dc):
        return (region, row + dr, col + dc)

    def out_copy(g, n, target):
        dr, dc, source, part = routes[n]
        if source < 2:
            src, dst = edge.at[source, g, :, part], strip.at[1 - source, g, :, part]
        elif source == 2:
            src, dst = own.at[g, :, pl.ds(rim, rim)], own.at[g, :, pl.ds(rim + tokens, rim)]
        else:
            src, dst = own.at[g, :, pl.ds(tokens, rim)], own.at[g, :, pl.ds(0, rim)]
        return pltpu.make_async_remote_copy(
            src_ref=src, dst_ref=dst, send_sem=send_sem.at[g, n], recv_sem=recv_sem.at[g, n],
            device_id=target, device_id_type=MESH)

    def back_copy(g, n, target):
        dr, dc, source, part = routes[n]
        if source < 2:
            src, dst = gstrip.at[1 - source, g, :, part], redge.at[source, g, :, part]
        else:
            src, dst = grow.at[3 - source, g], rrow.at[source - 2, g]
        return pltpu.make_async_remote_copy(
            src_ref=src, dst_ref=dst, send_sem=gsend_sem.at[g, n], recv_sem=grecv_sem.at[g, n],
            device_id=target, device_id_type=MESH)

    def load(g, n):
        lanes = pl.ds(g * width, width)
        if n < 2:
            src, dst = (k_hbm, v_hbm)[n], own.at[g, n, pl.ds(rim, tokens)]
        else:
            src, dst = (q_hbm, do_hbm)[n - 2], (q_ref, do_ref)[n - 2].at[g]
        return pltpu.make_async_copy(src.at[:, lanes], dst, load_sem.at[g, n])

    tables = [
        pltpu.make_async_copy(src, dst, table_sem.at[n])
        for n, (src, dst) in enumerate(((pick_hbm, pick_ref), (code_hbm, code_ref), (place_hbm, place_ref),
                                        (tissue_hbm, tissue_ref), (slide_hbm, slide_ref)))]
    tables[0].start()
    for g in range(groups):
        for n in range(2):
            load(g, n).start()
    for n in (1, 3, 4):
        tables[n].start()
    for g in range(groups):
        for n in range(2, 4):
            load(g, n).start()
    tables[2].start()

    zero_rim = jnp.zeros((groups, 2, rim, width), BF16)
    own[:, :, pl.ds(0, rim)] = zero_rim
    own[:, :, pl.ds(rim + tokens, rim)] = zero_rim
    strip[...] = jnp.zeros(strip.shape, BF16)
    redge[...] = jnp.zeros(redge.shape, BF16)
    rrow[...] = jnp.zeros(rrow.shape, BF16)

    barrier = pltpu.get_barrier_semaphore()
    around = jnp.int32(0)
    for dr in (-1, 0, 1):
        for dc in (-1, 0, 1):
            if dr or dc:
                good = exists(dr, dc)
                around = around + good.astype(jnp.int32)

                @pl.when(good)
                def _(dr=dr, dc=dc):
                    pl.semaphore_signal(barrier, inc=1, device_id=device(dr, dc), device_id_type=MESH)

    tables[0].wait()
    for g in range(groups):
        for i in range(2):
            load(g, i).wait()
            picked = dot(pick_ref[...], own[g, i, pl.ds(rim, tokens)], (1, 0)).astype(BF16)
            edge[0, g, i] = picked[:slots]
            edge[1, g, i] = picked[slots:]
        if g == 0:
            pl.semaphore_wait(barrier, around)
        for n, (dr, dc, _, _) in enumerate(routes):
            @pl.when(exists(dr, dc))
            def _(n=n, dr=dr, dc=dc):
                out_copy(g, n, device(dr, dc)).start()

    def label(r, c):
        c_all, r_all = tissue_ref.shape
        inside = (r >= 0) & (r < r_all) & (c >= 0) & (c < c_all)
        r, c = jnp.clip(r, 0, r_all - 1), jnp.clip(c, 0, c_all - 1)
        return jnp.where(inside & (tissue_ref[c, r] == 1), slide_ref[c, r] + 1, 0)

    tables[3].wait()
    tables[4].wait()
    labels = [[label(row * blocks + i - 1, col + j - 1) for j in range(3)] for i in range(blocks + 2)]
    tables[1].wait()
    for b in range(blocks):
        code = code_ref[b]
        mine = labels[b + 1][1]
        level = jnp.where(code == 9, 0.0, -1e30)
        for n in range(9):
            value = jnp.where((mine > 0) & (labels[b + n // 3][n % 3] == mine), 0.0, -1e30)
            level = jnp.where(code == n, value, level)
        bias[b] = level

    lane_head = lax.broadcasted_iota(jnp.int32, (per_block, width), 1) // depth

    def stack(block):
        zero = jnp.zeros_like(block)
        return jnp.concatenate([jnp.where(lane_head == h, block, zero) for h in range(stacked)], axis=0)

    def unstack(full):
        result = full[:per_block]
        for h in range(1, stacked):
            result = jnp.where(lane_head == h, full[h * per_block:(h + 1) * per_block], result)
        return result

    for g in range(groups):
        for n in range(2, 4):
            load(g, n).wait()
    tables[2].wait()

    def compute(g, carry):
        for n, (dr, dc, _, _) in enumerate(routes):
            @pl.when(exists(-dr, -dc))
            def _(n=n, dr=dr, dc=dc):
                out_copy(g, n, device(-dr, -dc)).wait_recv()
        lanes = pl.ds(pl.multiple_of(g * width, width), width)
        acc[g] = jnp.zeros(acc.shape[1:], F32)
        sacc[...] = jnp.zeros(sacc.shape, F32)
        for b in range(blocks):
            mine = pl.ds(b * per_block, per_block)
            near = pl.ds(b * per_block, 128)
            far = pl.ds(strip_start(b, rows), 64)
            scale = 1.0 / depth ** 0.5
            q = stack((q_ref[g, mine].astype(F32) * scale).astype(BF16))
            do = stack(do_ref[g, mine])
            keys, values = (
                jnp.concatenate([own[g, i, near], strip[0, g, i, far], strip[1, g, i, far]], axis=0)
                for i in range(2))
            scores = dot(keys, q, (1, 1)) + jnp.concatenate([bias[b]] * (stacked // 2), axis=1)
            highest = jnp.max(scores, axis=0, keepdims=True)
            powers = jnp.exp(scores - highest)
            total = jnp.sum(powers, axis=0, keepdims=True)
            weights = powers * (1.0 / total)
            soft = weights.astype(BF16)
            prob_grad = dot(values, do, (1, 1))
            delta = jnp.sum(weights * prob_grad, axis=0, keepdims=True)
            score_grad = (weights * (prob_grad - delta)).astype(BF16)
            att_ref[mine, lanes] = unstack(dot(soft, values, (0, 0))).astype(BF16)
            dq_ref[mine, lanes] = (unstack(dot(score_grad, keys, (0, 0))) * scale).astype(BF16)
            for i, part in enumerate((dot(score_grad, q, (1, 0)), dot(soft, do, (1, 0)))):
                acc[g, i, near] += part[:128]
                sacc[0, i, far] += part[128:192]
                sacc[1, i, far] += part[192:]
        grow[0, g] = acc[g, :, pl.ds(0, rim)].astype(BF16)
        grow[1, g] = acc[g, :, pl.ds(rim + tokens, rim)].astype(BF16)
        gstrip[:, g] = sacc[...].astype(BF16)
        for n, (dr, dc, _, _) in enumerate(routes):
            @pl.when(exists(-dr, -dc))
            def _(n=n, dr=dr, dc=dc):
                back_copy(g, n, device(-dr, -dc)).start()
        return carry

    lax.fori_loop(0, groups, compute, 0)

    def finish(g, carry):
        for n, (dr, dc, _, _) in enumerate(routes):
            @pl.when(exists(dr, dc))
            def _(n=n, dr=dr, dc=dc):
                out_copy(g, n, device(dr, dc)).wait_send()
                back_copy(g, n, device(dr, dc)).wait_recv()
        lanes = pl.ds(pl.multiple_of(g * width, width), width)
        for i, ref in enumerate((dk_ref, dv_ref)):
            edges = jnp.concatenate([redge[0, g, i], redge[1, g, i]], axis=0)
            acc[g, i, pl.ds(rim, rim)] += rrow[0, g, i].astype(F32)
            acc[g, i, pl.ds(tokens, rim)] += rrow[1, g, i].astype(F32)
            total = acc[g, i, pl.ds(rim, tokens)] + dot(place_ref[...], edges, (1, 0))
            ref[:, lanes] = total.astype(BF16)
        for n, (dr, dc, _, _) in enumerate(routes):
            @pl.when(exists(-dr, -dc))
            def _(n=n, dr=dr, dc=dc):
                back_copy(g, n, device(-dr, -dc)).wait_send()
        return carry

    lax.fori_loop(0, groups, finish, 0)


def write_out(*refs):
    copies = [pltpu.make_async_copy(refs[n], refs[4 + n], refs[8].at[n]) for n in range(4)]
    for copy in copies:
        copy.start()
    for copy in copies:
        copy.wait()


def local(queries, key_states, value_states, out_grad, tissue, slide_id):
    rows, cols, feature = queries.shape
    depth = feature // HEADS
    stacked = 4
    width = stacked * depth
    groups = feature // width
    tokens = rows * cols
    rim = RIM * cols
    slots = REACH * rows + 2 * PACK
    sizes = (rows, cols, groups, width, depth, lax.axis_size("row"), lax.axis_size("col"))
    picks = edge_picks(rows, cols)
    flat = [pltpu.with_memory_space_constraint(a.reshape(tokens, feature), pltpu.HBM) for a in (queries, key_states, value_states, out_grad)]
    vmem = pl.BlockSpec(memory_space=pltpu.VMEM)
    hbm = pl.BlockSpec(memory_space=pltpu.HBM)
    blocks = rows // LABEL
    outs = pl.pallas_call(
        functools.partial(kernel, sizes),
        out_shape=[pltpu.VMEM((tokens, feature), BF16)] * 4,
        in_specs=[hbm] * 4 + [hbm] * 2 + [hbm] * 3,
        out_specs=[vmem] * 4,
        scratch_shapes=[
            pltpu.SMEM(tissue.shape[::-1], jnp.int32),
            pltpu.SMEM(tissue.shape[::-1], jnp.int32),
            pltpu.VMEM((groups, tokens, width), BF16),
            pltpu.VMEM((groups, tokens, width), BF16),
            pltpu.VMEM((blocks, 256, 2 * LABEL * cols), F32),
            pltpu.VMEM((2 * slots, tokens), BF16),
            pltpu.VMEM((tokens, 2 * slots), BF16),
            pltpu.VMEM((groups, 2, tokens + 2 * rim, width), BF16),
            pltpu.VMEM((2, groups, 2, slots, width), BF16),
            pltpu.VMEM((2, groups, 2, slots, width), BF16),
            pltpu.VMEM((2, groups, 2, rim, width), BF16),
            pltpu.VMEM((2, groups, 2, slots, width), BF16),
            pltpu.VMEM((2, groups, 2, rim, width), BF16),
            pltpu.VMEM((2, groups, 2, slots, width), BF16),
            pltpu.VMEM((groups, 2, tokens + 2 * rim, width), F32),
            pltpu.VMEM((2, 2, slots, width), F32),
            pltpu.VMEM((blocks, 256, 2 * LABEL * cols), F32),
            pltpu.SemaphoreType.DMA((groups, 8)),
            pltpu.SemaphoreType.DMA((groups, 8)),
            pltpu.SemaphoreType.DMA((groups, 8)),
            pltpu.SemaphoreType.DMA((groups, 8)),
            pltpu.SemaphoreType.DMA((groups, 4)),
            pltpu.SemaphoreType.DMA((5,)),
        ],
        compiler_params=pltpu.CompilerParams(
            collective_id=0, has_side_effects=True, vmem_limit_bytes=40 * 2 ** 20),
        name="window_attention",
    )(
        *flat,
        *[pltpu.with_memory_space_constraint(a.T, pltpu.HBM) for a in (tissue, slide_id)],
        *[pltpu.with_memory_space_constraint(a, pltpu.HBM) for a in (jnp.asarray(pair_codes(rows, cols)),
        jnp.asarray(picks, BF16),
        jnp.asarray(picks.T, BF16))],
    )
    outs = pl.pallas_call(
        write_out,
        out_shape=[jax.ShapeDtypeStruct((tokens, feature), BF16)] * 4,
        in_specs=[vmem] * 4,
        out_specs=[hbm] * 4,
        scratch_shapes=[pltpu.SemaphoreType.DMA((4,))],
        name="write_out",
    )(*[pltpu.with_memory_space_constraint(a, pltpu.VMEM) for a in outs])
    return tuple(a.reshape(rows, cols, feature) for a in outs)


def solution(mesh):
    tile = P(("region", "row"), "col", None)
    table = P("region", None)
    return jax.shard_map(
        local,
        mesh=mesh,
        in_specs=(tile,) * 4 + (table,) * 2,
        out_specs=(tile,) * 4,
        check_vma=False,
    )
```

```python
import functools

import jax
import jax.numpy as jnp
import numpy as np
from jax import lax
from jax.experimental import pallas as pl
from jax.experimental.pallas import tpu as pltpu
from jax.sharding import PartitionSpec as P

HEADS = 12
LABEL = 8
REACH = 3
RIM = 4
PACK = 16
MESH = pl.DeviceIdType.MESH
BF16 = jnp.bfloat16
F32 = jnp.float32


def edge_places(rows):
    places = [None] * (2 * PACK + REACH * rows)
    for t in range(RIM * REACH):
        places[t] = (t // REACH - RIM, t % REACH)
        places[PACK + REACH * rows + t] = (rows + t // REACH, t % REACH)
    for t in range(REACH * rows):
        places[PACK + t] = (t // REACH, t % REACH)
    return places


def strip_start(block, rows):
    return min((LABEL * REACH * block + PACK - RIM * REACH) // PACK * PACK, REACH * rows + 2 * PACK - 64)


def edge_picks(rows, cols):
    places = edge_places(rows)
    picks = np.zeros((2, len(places), rows * cols), np.float32)
    for slot, place in enumerate(places):
        if place is not None:
            row, j = place
            picks[0, slot, (row % rows) * cols + j] = 1
            picks[1, slot, (row % rows) * cols + cols - REACH + j] = 1
    return picks.reshape(2 * len(places), rows * cols)


def pair_codes(rows, cols):
    places = edge_places(rows)
    blocks = rows // LABEL
    codes = np.full((blocks, LABEL * cols, 128 + 128), -1, np.float32)
    for b in range(blocks):
        keys = [((LABEL * cols * b + s) // cols - RIM, s % cols) for s in range(128)]
        first = strip_start(b, rows)
        for shift in (-REACH, cols):
            for s in range(64):
                place = places[first + s]
                keys.append(None if place is None else (place[0], place[1] + shift))
        for q in range(LABEL * cols):
            row, col = LABEL * b + q // cols, q % cols
            for n, key in enumerate(keys):
                if key is None or abs(key[0] - row) > REACH or abs(key[1] - col) > REACH:
                    continue
                if key == (row, col):
                    codes[b, q, n] = 9
                else:
                    codes[b, q, n] = (key[0] // LABEL - b + 1) * 3 + key[1] // LABEL + 1
    return np.tile(codes.transpose(0, 2, 1), (1, 1, 2))


def dot(a, b, contract):
    return lax.dot_general(a, b, ((contract[:1], contract[1:]), ((), ())), preferred_element_type=F32)


def kernel(
    sizes,
    q_hbm, k_hbm, v_hbm, do_hbm, tissue_hbm, slide_hbm, code_hbm, pick_hbm, place_hbm,
    att_ref, dq_ref, dk_ref, dv_ref,
    tissue_ref, slide_ref, q_ref, do_ref, code_ref, pick_ref, place_ref, own, strip, edge, grow, gstrip, rrow, redge, acc, sacc, bias,
    send_sem, recv_sem, gsend_sem, grecv_sem, load_sem, table_sem,
):
    rows, cols, groups, width, depth, row_size, col_size = sizes
    tokens = rows * cols
    rim = RIM * cols
    side = REACH * rows
    slots = side + 2 * PACK
    blocks = rows // LABEL
    per_block = LABEL * cols
    stacked = width // depth
    region, row, col = lax.axis_index("region"), lax.axis_index("row"), lax.axis_index("col")

    top, mid, bottom = pl.ds(0, PACK), pl.ds(PACK, side), pl.ds(PACK + side, PACK)
    routes = []
    routes.append((-1, 0, 2, None))
    routes.append((1, 0, 3, None))
    for source, dc in ((0, -1), (1, 1)):
        routes.append((1, dc, source, top))
        routes.append((-1, dc, source, bottom))
    routes.append((0, -1, 0, mid))
    routes.append((0, 1, 1, mid))

    def exists(dr, dc):
        good = None
        for at, d, size in ((row, dr, row_size), (col, dc, col_size)):
            if d:
                here = (at + d >= 0) if d < 0 else (at + d < size)
                good = here if good is None else good & here
        return good

    def device(dr, dc):
        return (region, row + dr, col + dc)

    def out_copy(g, n, target):
        dr, dc, source, part = routes[n]
        if source < 2:
            src, dst = edge.at[source, g, :, part], strip.at[1 - source, g, :, part]
        elif source == 2:
            src, dst = own.at[g, :, pl.ds(rim, rim)], own.at[g, :, pl.ds(rim + tokens, rim)]
        else:
            src, dst = own.at[g, :, pl.ds(tokens, rim)], own.at[g, :, pl.ds(0, rim)]
        return pltpu.make_async_remote_copy(
            src_ref=src, dst_ref=dst, send_sem=send_sem.at[g, n], recv_sem=recv_sem.at[g, n],
            device_id=target, device_id_type=MESH)

    def back_copy(g, n, target):
        dr, dc, source, part = routes[n]
        if source < 2:
            src, dst = gstrip.at[1 - source, g, :, part], redge.at[source, g, :, part]
        else:
            src, dst = grow.at[3 - source, g], rrow.at[source - 2, g]
        return pltpu.make_async_remote_copy(
            src_ref=src, dst_ref=dst, send_sem=gsend_sem.at[g, n], recv_sem=grecv_sem.at[g, n],
            device_id=target, device_id_type=MESH)

    def load(g, n):
        lanes = pl.ds(g * width, width)
        if n < 2:
            src, dst = (k_hbm, v_hbm)[n], own.at[g, n, pl.ds(rim, tokens)]
        else:
            src, dst = (q_hbm, do_hbm)[n - 2], (q_ref, do_ref)[n - 2].at[g]
        return pltpu.make_async_copy(src.at[:, lanes], dst, load_sem.at[g, n])

    tables = [
        pltpu.make_async_copy(src, dst, table_sem.at[n])
        for n, (src, dst) in enumerate(((pick_hbm, pick_ref), (code_hbm, code_ref), (place_hbm, place_ref),
                                        (tissue_hbm, tissue_ref), (slide_hbm, slide_ref)))]
    tables[0].start()
    for g in range(groups):
        for n in range(2):
            load(g, n).start()
    for n in (1, 3, 4):
        tables[n].start()
    for g in range(groups):
        for n in range(2, 4):
            load(g, n).start()
    tables[2].start()

    zero_rim = jnp.zeros((groups, 2, rim, width), BF16)
    own[:, :, pl.ds(0, rim)] = zero_rim
    own[:, :, pl.ds(rim + tokens, rim)] = zero_rim
    strip[...] = jnp.zeros(strip.shape, BF16)
    redge[...] = jnp.zeros(redge.shape, BF16)
    rrow[...] = jnp.zeros(rrow.shape, BF16)

    barrier = pltpu.get_barrier_semaphore()
    around = jnp.int32(0)
    for dr in (-1, 0, 1):
        for dc in (-1, 0, 1):
            if dr or dc:
                good = exists(dr, dc)
                around = around + good.astype(jnp.int32)

                @pl.when(good)
                def _(dr=dr, dc=dc):
                    pl.semaphore_signal(barrier, inc=1, device_id=device(dr, dc), device_id_type=MESH)

    tables[0].wait()
    for g in range(groups):
        for i in range(2):
            load(g, i).wait()
            picked = dot(pick_ref[...], own[g, i, pl.ds(rim, tokens)], (1, 0)).astype(BF16)
            edge[0, g, i] = picked[:slots]
            edge[1, g, i] = picked[slots:]
        if g == 0:
            pl.semaphore_wait(barrier, around)
        for n, (dr, dc, _, _) in enumerate(routes):
            @pl.when(exists(dr, dc))
            def _(n=n, dr=dr, dc=dc):
                out_copy(g, n, device(dr, dc)).start()

    def label(r, c):
        c_all, r_all = tissue_ref.shape
        inside = (r >= 0) & (r < r_all) & (c >= 0) & (c < c_all)
        r, c = jnp.clip(r, 0, r_all - 1), jnp.clip(c, 0, c_all - 1)
        return jnp.where(inside & (tissue_ref[c, r] == 1), slide_ref[c, r] + 1, 0)

    tables[3].wait()
    tables[4].wait()
    labels = [[label(row * blocks + i - 1, col + j - 1) for j in range(3)] for i in range(blocks + 2)]
    tables[1].wait()
    for b in range(blocks):
        code = code_ref[b]
        mine = labels[b + 1][1]
        level = jnp.where(code == 9, 0.0, -1e30)
        for n in range(9):
            value = jnp.where((mine > 0) & (labels[b + n // 3][n % 3] == mine), 0.0, -1e30)
            level = jnp.where(code == n, value, level)
        bias[b] = level

    lane_head = lax.broadcasted_iota(jnp.int32, (per_block, width), 1) // depth

    def stack(block):
        zero = jnp.zeros_like(block)
        return jnp.concatenate([jnp.where(lane_head == h, block, zero) for h in range(stacked)], axis=0)

    def unstack(full):
        result = full[:per_block]
        for h in range(1, stacked):
            result = jnp.where(lane_head == h, full[h * per_block:(h + 1) * per_block], result)
        return result

    for g in range(groups):
        for n in range(2, 4):
            load(g, n).wait()
    tables[2].wait()

    def compute(g, carry):
        for n, (dr, dc, _, part) in enumerate(routes):
            if part is mid:
                @pl.when(exists(-dr, -dc))
                def _(n=n, dr=dr, dc=dc):
                    out_copy(g, n, device(-dr, -dc)).wait_recv()
        lanes = pl.ds(pl.multiple_of(g * width, width), width)
        acc[g] = jnp.zeros(acc.shape[1:], F32)
        sacc[...] = jnp.zeros(sacc.shape, F32)
        for b in [*range(1, blocks - 1), blocks - 1, 0]:
            if b == blocks - 1:
                for n, (dr, dc, _, part) in enumerate(routes):
                    if part is not mid:
                        @pl.when(exists(-dr, -dc))
                        def _(n=n, dr=dr, dc=dc):
                            out_copy(g, n, device(-dr, -dc)).wait_recv()
            mine = pl.ds(b * per_block, per_block)
            near = pl.ds(b * per_block, 128)
            far = pl.ds(strip_start(b, rows), 64)
            scale = 1.0 / depth ** 0.5
            q = stack((q_ref[g, mine].astype(F32) * scale).astype(BF16))
            do = stack(do_ref[g, mine])
            keys, values = (
                jnp.concatenate([own[g, i, near], strip[0, g, i, far], strip[1, g, i, far]], axis=0)
                for i in range(2))
            scores = dot(keys, q, (1, 1)) + jnp.concatenate([bias[b]] * (stacked // 2), axis=1)
            highest = jnp.max(scores, axis=0, keepdims=True)
            powers = jnp.exp(scores - highest)
            total = jnp.sum(powers, axis=0, keepdims=True)
            weights = powers * (1.0 / total)
            soft = weights.astype(BF16)
            prob_grad = dot(values, do, (1, 1))
            delta = jnp.sum(weights * prob_grad, axis=0, keepdims=True)
            score_grad = (weights * (prob_grad - delta)).astype(BF16)
            att_ref[mine, lanes] = unstack(dot(soft, values, (0, 0))).astype(BF16)
            dq_ref[mine, lanes] = (unstack(dot(score_grad, keys, (0, 0))) * scale).astype(BF16)
            for i, part in enumerate((dot(score_grad, q, (1, 0)), dot(soft, do, (1, 0)))):
                acc[g, i, near] += part[:128]
                sacc[0, i, far] += part[128:192]
                sacc[1, i, far] += part[192:]
        grow[0, g] = acc[g, :, pl.ds(0, rim)].astype(BF16)
        grow[1, g] = acc[g, :, pl.ds(rim + tokens, rim)].astype(BF16)
        gstrip[:, g] = sacc[...].astype(BF16)
        for n, (dr, dc, _, _) in enumerate(routes):
            @pl.when(exists(-dr, -dc))
            def _(n=n, dr=dr, dc=dc):
                back_copy(g, n, device(-dr, -dc)).start()
        return carry

    lax.fori_loop(0, groups, compute, 0)

    def finish(g, carry):
        for n, (dr, dc, _, _) in enumerate(routes):
            @pl.when(exists(dr, dc))
            def _(n=n, dr=dr, dc=dc):
                out_copy(g, n, device(dr, dc)).wait_send()
                back_copy(g, n, device(dr, dc)).wait_recv()
        lanes = pl.ds(pl.multiple_of(g * width, width), width)
        for i, ref in enumerate((dk_ref, dv_ref)):
            edges = jnp.concatenate([redge[0, g, i], redge[1, g, i]], axis=0)
            acc[g, i, pl.ds(rim, rim)] += rrow[0, g, i].astype(F32)
            acc[g, i, pl.ds(tokens, rim)] += rrow[1, g, i].astype(F32)
            total = acc[g, i, pl.ds(rim, tokens)] + dot(place_ref[...], edges, (1, 0))
            ref[:, lanes] = total.astype(BF16)
        for n, (dr, dc, _, _) in enumerate(routes):
            @pl.when(exists(-dr, -dc))
            def _(n=n, dr=dr, dc=dc):
                back_copy(g, n, device(-dr, -dc)).wait_send()
        return carry

    lax.fori_loop(0, groups, finish, 0)


def write_out(*refs):
    copies = [pltpu.make_async_copy(refs[n], refs[4 + n], refs[8].at[n]) for n in range(4)]
    for copy in copies:
        copy.start()
    for copy in copies:
        copy.wait()


def local(queries, key_states, value_states, out_grad, tissue, slide_id):
    rows, cols, feature = queries.shape
    depth = feature // HEADS
    stacked = 4
    width = stacked * depth
    groups = feature // width
    tokens = rows * cols
    rim = RIM * cols
    slots = REACH * rows + 2 * PACK
    sizes = (rows, cols, groups, width, depth, lax.axis_size("row"), lax.axis_size("col"))
    picks = edge_picks(rows, cols)
    flat = [pltpu.with_memory_space_constraint(a.reshape(tokens, feature), pltpu.HBM) for a in (queries, key_states, value_states, out_grad)]
    vmem = pl.BlockSpec(memory_space=pltpu.VMEM)
    hbm = pl.BlockSpec(memory_space=pltpu.HBM)
    blocks = rows // LABEL
    outs = pl.pallas_call(
        functools.partial(kernel, sizes),
        out_shape=[pltpu.VMEM((tokens, feature), BF16)] * 4,
        in_specs=[hbm] * 4 + [hbm] * 2 + [hbm] * 3,
        out_specs=[vmem] * 4,
        scratch_shapes=[
            pltpu.SMEM(tissue.shape[::-1], jnp.int32),
            pltpu.SMEM(tissue.shape[::-1], jnp.int32),
            pltpu.VMEM((groups, tokens, width), BF16),
            pltpu.VMEM((groups, tokens, width), BF16),
            pltpu.VMEM((blocks, 256, 2 * LABEL * cols), F32),
            pltpu.VMEM((2 * slots, tokens), BF16),
            pltpu.VMEM((tokens, 2 * slots), BF16),
            pltpu.VMEM((groups, 2, tokens + 2 * rim, width), BF16),
            pltpu.VMEM((2, groups, 2, slots, width), BF16),
            pltpu.VMEM((2, groups, 2, slots, width), BF16),
            pltpu.VMEM((2, groups, 2, rim, width), BF16),
            pltpu.VMEM((2, groups, 2, slots, width), BF16),
            pltpu.VMEM((2, groups, 2, rim, width), BF16),
            pltpu.VMEM((2, groups, 2, slots, width), BF16),
            pltpu.VMEM((groups, 2, tokens + 2 * rim, width), F32),
            pltpu.VMEM((2, 2, slots, width), F32),
            pltpu.VMEM((blocks, 256, 2 * LABEL * cols), F32),
            pltpu.SemaphoreType.DMA((groups, 8)),
            pltpu.SemaphoreType.DMA((groups, 8)),
            pltpu.SemaphoreType.DMA((groups, 8)),
            pltpu.SemaphoreType.DMA((groups, 8)),
            pltpu.SemaphoreType.DMA((groups, 4)),
            pltpu.SemaphoreType.DMA((5,)),
        ],
        compiler_params=pltpu.CompilerParams(
            collective_id=0, has_side_effects=True, vmem_limit_bytes=40 * 2 ** 20),
        name="window_attention",
    )(
        *flat,
        *[pltpu.with_memory_space_constraint(a.T, pltpu.HBM) for a in (tissue, slide_id)],
        *[pltpu.with_memory_space_constraint(a, pltpu.HBM) for a in (jnp.asarray(pair_codes(rows, cols)),
        jnp.asarray(picks, BF16),
        jnp.asarray(picks.T, BF16))],
    )
    outs = pl.pallas_call(
        write_out,
        out_shape=[jax.ShapeDtypeStruct((tokens, feature), BF16)] * 4,
        in_specs=[vmem] * 4,
        out_specs=[hbm] * 4,
        scratch_shapes=[pltpu.SemaphoreType.DMA((4,))],
        name="write_out",
    )(*[pltpu.with_memory_space_constraint(a, pltpu.VMEM) for a in outs])
    return tuple(a.reshape(rows, cols, feature) for a in outs)


def solution(mesh):
    tile = P(("region", "row"), "col", None)
    table = P("region", None)
    return jax.shard_map(
        local,
        mesh=mesh,
        in_specs=(tile,) * 4 + (table,) * 2,
        out_specs=(tile,) * 4,
        check_vma=False,
    )
```
